32 devices in a mesh: dp: 16 (over z, y, core), tensor: 2 (over x).
Axes of the slice: x: 2, y: 2, z: 4, core: 2. Of those that a mesh axis runs over, the one named last changes fastest.
Arguments:
- hidden_in: bfloat16 [16384, 1024], P(('dp', 'tensor')), may hold values from -6 to 6
- w_z: bfloat16 [2, 1024, 2048], P(None, 'dp', 'tensor'), may hold values from -0.1875 to 0.1875
- w_x: bfloat16 [2, 1024, 2048], P(None, 'dp', 'tensor'), may hold values from -0.1875 to 0.1875
- w_dt: bfloat16 [2, 1024, 32], P(None, 'dp', 'tensor'), may hold values from -0.1875 to 0.1875
- w_bc: bfloat16 [2, 1024, 256], P(None, ('dp', 'tensor')), may hold values from -0.1875 to 0.1875
- w_out: bfloat16 [2, 2048, 1024], P(None, 'tensor', 'dp'), may hold values from -0.125 to 0.125
- conv_x: float32 [2, 4, 2048], P(None, None, 'tensor'), may hold values from -3 to 3
- conv_bc: float32 [2, 4, 256], replicated, may hold values from -3 to 3
- bias_x: float32 [2, 2048], P(None, 'tensor'), may hold values from -0.5 to 0.5
- bias_bc: float32 [2, 256], replicated, may hold values from -0.5 to 0.5
- dt_bias: float32 [2, 32], P(None, 'tensor'), may hold values from -4 to -1
- a_log: float32 [2, 32], P(None, 'tensor'), may hold values from -3 to 1.5
- d_skip: float32 [2, 32], P(None, 'tensor'), may hold values from 0.5 to 1.5
- gate_gain: float32 [2, 2048], P(None, 'tensor'), may hold values from 0.5 to 1.5
- pre_gain: float32 [2, 1024], replicated, may hold values from 0.5 to 1.5
- seq_lengths: int32 [16, 4], P('dp'), may hold values from 0 to 1024, as said below
- cotangent: bfloat16 [16384, 1024], P(('dp', 'tensor')), may hold values from -6 to 6
Outputs:
- hidden_out: bfloat16 [16384, 1024], P(('dp', 'tensor'))
- grad_hidden: float32 [16384, 1024], P(('dp', 'tensor'))
- grad_w_z: float32 [2, 1024, 2048], P(None, 'dp', 'tensor')
- grad_w_x: float32 [2, 1024, 2048], P(None, 'dp', 'tensor')
- grad_w_dt: float32 [2, 1024, 32], P(None, 'dp', 'tensor')
- grad_w_bc: float32 [2, 1024, 256], P(None, ('dp', 'tensor'))
- grad_w_out: float32 [2, 2048, 1024], P(None, 'tensor', 'dp')
- grad_conv_x: float32 [2, 4, 2048], P(None, None, 'tensor')
- grad_conv_bc: float32 [2, 4, 256], replicated
- grad_bias_x: float32 [2, 2048], P(None, 'tensor')
- grad_bias_bc: float32 [2, 256], replicated
- grad_dt_bias: float32 [2, 32], P(None, 'tensor')
- grad_a_log: float32 [2, 32], P(None, 'tensor')
- grad_d_skip: float32 [2, 32], P(None, 'tensor')
- grad_gate_gain: float32 [2, 2048], P(None, 'tensor')
- grad_pre_gain: float32 [2, 1024], replicated
The draws below stay inside these ranges and needn't reach their ends.
Inputs may be any that keep to these rules, and one draw needn't show every extreme that they name: `seq_lengths`: row g lists the lengths of the sequences packed, in slot order from the first slot, into dp group g's 1024 token slots; a row sums to at most 1024 and the slots after its sum are padding; a length may be 0; in every draw some row is a single sequence of 1024 tokens.
All inputs are finite; a program needn't handle non-finite values.
Results may differ from the reference program's by a relative error of at most 0.024.
Values may be sent and summed in bfloat16 or wider, within the bound.
A program may use at most 320 MiB of HBM per device.

```python
from functools import partial
import jax
import jax.numpy as jnp
from jax import lax

D = 1024
INNER = 2048
HEADS = 32
STATE = 128
CONV = 4
SPAN = 256
LAYERS = 2
SLOTS = 4
TOK_GRP = 1024
GROUPS = 16
TOKENS = 16384
N_TENSOR = 2


def draw_seq_lengths(key, part):
    first_key, second_key, third_key = jax.random.split(key, 3)
    totals = jax.random.randint(first_key, (GROUPS,), TOK_GRP // 2, TOK_GRP + 1).astype(jnp.int32)
    cuts = jnp.sort(jax.random.randint(second_key, (GROUPS, SLOTS - 1), 0, TOK_GRP + 1).astype(jnp.int32), axis=1)
    cuts = jnp.minimum(cuts, totals[:, None])
    edges = jnp.concatenate([jnp.zeros((GROUPS, 1), jnp.int32), cuts, totals[:, None]], axis=1)
    lengths = edges[:, 1:] - edges[:, :-1]
    chosen = jax.random.randint(third_key, (), 0, GROUPS).astype(jnp.int32)
    single = jnp.concatenate([jnp.full((1,), TOK_GRP, jnp.int32), jnp.zeros((SLOTS - 1,), jnp.int32)])
    rows = jnp.arange(GROUPS, dtype=jnp.int32)
    lengths = jnp.where((rows == chosen)[:, None], single[None, :], lengths)
    return lengths.astype(jnp.int32)


def block_levels(stream_key, dims, cuts, least, largest):
    def one(position, parts):
        heights = jax.random.uniform(jax.random.fold_in(jax.random.fold_in(stream_key, 6), position), (parts,), jnp.float32, least / len(cuts), largest / len(cuts))
        return jnp.repeat(jnp.exp(heights), dims[position] // parts).reshape((-1,) + (1,) * (len(dims) - position - 1))

    level = one(*cuts[0])
    for cut in cuts[1:]:
        level = level * one(*cut)
    return level


def normal_values(stream_key, dims, scale, bound, shards=(), kind=jnp.bfloat16):
    array = scale * jax.random.normal(stream_key, dims, jnp.float32)
    if shards:
        array = array * block_levels(stream_key, dims, shards, -0.22, 0.18)
    return jnp.clip(array, -bound, bound).astype(kind)


def setup_inputs(seed: int = 0) -> dict:
    keys = jax.random.split(jax.random.key(seed), 18)
    hidden_in = normal_values(keys[0], (TOKENS, D), 1.0, 6.0, ((0, 32),))
    w_z = normal_values(keys[1], (LAYERS, D, INNER), D ** -0.5, 0.1875, ((1, 16), (2, 2)))
    w_x = normal_values(keys[2], (LAYERS, D, INNER), D ** -0.5, 0.1875, ((1, 16), (2, 2)))
    w_dt = normal_values(keys[3], (LAYERS, D, HEADS), D ** -0.5, 0.1875, ((1, 16), (2, 2)))
    w_bc = normal_values(keys[4], (LAYERS, D, 2 * STATE), D ** -0.5, 0.1875, ((1, 32),))
    w_out = normal_values(keys[5], (LAYERS, INNER, D), INNER ** -0.5, 0.125, ((1, 2), (2, 16)))
    conv_x = normal_values(keys[6], (LAYERS, CONV, INNER), CONV ** -0.5, 3.0, ((2, 2),), jnp.float32)
    conv_bc = normal_values(keys[7], (LAYERS, CONV, 2 * STATE), CONV ** -0.5, 3.0, (), jnp.float32)
    bias_x = jnp.clip(jax.random.uniform(keys[8], (LAYERS, INNER), jnp.float32, -0.5, 0.5) * block_levels(keys[8], (LAYERS, INNER), ((1, 2),), -0.4, 0.0), -0.5, 0.5)
    bias_bc = jnp.clip(jax.random.uniform(keys[9], (LAYERS, 2 * STATE), jnp.float32, -0.5, 0.5), -0.5, 0.5)
    dt_bias = jnp.clip(-4.0 + 3.0 * jax.random.uniform(keys[10], (LAYERS, HEADS), jnp.float32) ** block_levels(keys[10], (LAYERS, HEADS), ((1, 2),), -0.2, 0.2), -4.0, -1.0)
    a_log = jnp.clip(-3.0 + 4.5 * jax.random.uniform(keys[11], (LAYERS, HEADS), jnp.float32) ** block_levels(keys[11], (LAYERS, HEADS), ((1, 2),), -0.2, 0.2), -3.0, 1.5)
    d_skip = jnp.clip(0.5 + 1.0 * jax.random.uniform(keys[12], (LAYERS, HEADS), jnp.float32) ** block_levels(keys[12], (LAYERS, HEADS), ((1, 2),), -0.2, 0.2), 0.5, 1.5)
    gate_gain = jnp.clip(1.0 + 0.1 * jax.random.normal(keys[13], (LAYERS, INNER), jnp.float32), 0.5, 1.5)
    pre_gain = jnp.clip(1.0 + 0.1 * jax.random.normal(keys[14], (LAYERS, D), jnp.float32), 0.5, 1.5)
    seq_lengths = draw_seq_lengths(jax.random.fold_in(keys[17], 71), 0)
    cotangent = normal_values(keys[16], (TOKENS, D), 1.0, 6.0, ((0, 32),))
    return dict(hidden_in=hidden_in, w_z=w_z, w_x=w_x, w_dt=w_dt, w_bc=w_bc, w_out=w_out, conv_x=conv_x, conv_bc=conv_bc, bias_x=bias_x, bias_bc=bias_bc, dt_bias=dt_bias, a_log=a_log, d_skip=d_skip, gate_gain=gate_gain, pre_gain=pre_gain, seq_lengths=seq_lengths, cotangent=cotangent)


epsilon = 1e-05
highest = lax.Precision.HIGHEST

def segment_ids(lengths, count):
    ends = jnp.cumsum(lengths).astype(jnp.int32)
    places = jnp.arange(count, dtype=jnp.int32)
    return lax.optimization_barrier(jnp.sum((places[:, None] >= ends[None, :]).astype(jnp.int32), axis=1)).astype(jnp.int32)

def causal_conv(values, kernel, offset, seg_ids):
    total = offset[None, :] + kernel[-1][None, :] * values
    for back_step in range(1, kernel.shape[0]):
        moved = jnp.concatenate([jnp.zeros((back_step, values.shape[1]), jnp.float32), values[:-back_step]], axis=0)
        moved_ids = jnp.concatenate([jnp.full((back_step,), -1, jnp.int32), seg_ids[:-back_step]])
        same_seq = (moved_ids == seg_ids).astype(jnp.float32)
        total = total + kernel[-1 - back_step][None, :] * moved * same_seq[:, None]
    return total

def state_scan(channels, step_sizes, decay_rate, b_mat, c_mat, seg_ids, block_len):
    count, nheads = step_sizes.shape
    head_width = channels.shape[1] // nheads
    nstate = b_mat.shape[1]
    nblocks = count // block_len
    xs = channels.reshape(nblocks, block_len, nheads, head_width)
    steps_h = jnp.transpose(step_sizes.reshape(nblocks, block_len, nheads), (0, 2, 1))
    bs = b_mat.reshape(nblocks, block_len, nstate)
    cs = c_mat.reshape(nblocks, block_len, nstate)
    ids = seg_ids.reshape(nblocks, block_len)
    cumul = jnp.cumsum(steps_h * decay_rate[None, :, None], axis=2)
    scores = jnp.einsum('cin,cjn->cij', cs, bs, precision=highest)
    places = jnp.arange(block_len)
    allowed = (ids[:, :, None] == ids[:, None, :]) & (places[:, None] >= places[None, :])[None]
    spread = cumul[:, :, :, None] - cumul[:, :, None, :]
    decay = jnp.exp(jnp.where(allowed[:, None, :, :], spread, -1e+30))
    mixing = scores[:, None, :, :] * decay * steps_h[:, :, None, :]
    inside = jnp.einsum('chij,cjhp->cihp', mixing, xs, precision=highest)
    last_ids = ids[:, -1]
    tail = jnp.exp(jnp.where((ids == last_ids[:, None])[:, None, :], cumul[:, :, -1:] - cumul, -1e+30)) * steps_h
    fresh = jnp.einsum('chj,cjn,cjhp->chpn', tail, bs, xs, precision=highest)
    prev_ids = jnp.concatenate([jnp.full((1,), -1, jnp.int32), last_ids[:-1]])
    keep_flag = (last_ids == prev_ids).astype(jnp.float32)
    carry_decay = jnp.exp(cumul[:, :, -1]) * keep_flag[:, None]

    def advance(state, inputs):
        factor, newer = inputs
        return (factor[:, None, None] * state + newer, state)
    _, before = lax.scan(advance, jnp.zeros((nheads, head_width, nstate), jnp.float32), (carry_decay, fresh))
    reach = jnp.exp(cumul) * (ids == prev_ids[:, None]).astype(jnp.float32)[:, None, :]
    outside = jnp.einsum('cin,chpn->cihp', cs, before, precision=highest) * jnp.transpose(reach, (0, 2, 1))[..., None]
    return (inside + outside).reshape(count, nheads * head_width)

def mixer_core(proj_x, proj_bc, proj_dt, conv_x, bias_x, conv_bc, bias_bc, dt_bias, a_log, d_skip, seg_ids, block_len):
    x_conv = jax.nn.silu(causal_conv(proj_x, conv_x, bias_x, seg_ids))
    bc_conv = jax.nn.silu(causal_conv(proj_bc, conv_bc, bias_bc, seg_ids))
    nstate = bc_conv.shape[1] // 2
    step_sizes = jax.nn.softplus(proj_dt + dt_bias[None, :])
    head_width = x_conv.shape[1] // step_sizes.shape[1]
    scanned = state_scan(x_conv, step_sizes, -jnp.exp(a_log), bc_conv[:, :nstate], bc_conv[:, nstate:], seg_ids, block_len)
    return scanned + jnp.repeat(d_skip, head_width)[None, :] * x_conv

def group_pass(hidden, cotan, lengths, params):
    w_z, w_x, w_dt, w_bc, w_out, conv_x, conv_bc, bias_x, bias_bc, dt_bias, a_log, d_skip, gate_gain, pre_gain = params
    seg_ids = segment_ids(lengths, TOK_GRP)
    live = (seg_ids < SLOTS).astype(jnp.float32)
    inner_part = INNER // N_TENSOR
    head_part = HEADS // N_TENSOR
    stream = hidden.astype(jnp.float32)
    stored = []
    for layer_index in range(LAYERS):
        scale_pre = lax.rsqrt(lax.optimization_barrier(jnp.mean(stream * stream, axis=1)) + epsilon)
        normed = (stream * scale_pre[:, None] * pre_gain[layer_index][None, :]).astype(jnp.bfloat16)
        gate_raw = jnp.dot(normed, w_z[layer_index], preferred_element_type=jnp.float32)
        proj_x = jnp.dot(normed, w_x[layer_index], preferred_element_type=jnp.float32)
        proj_dt = jnp.dot(normed, w_dt[layer_index], preferred_element_type=jnp.float32)
        proj_bc = jnp.dot(normed, w_bc[layer_index], preferred_element_type=jnp.float32)
        outputs_list = []
        backs = []
        for group_index in range(N_TENSOR):
            chan_cut = slice(group_index * inner_part, (group_index + 1) * inner_part)
            head_cut = slice(group_index * head_part, (group_index + 1) * head_part)
            mixed_part, back_part = jax.vjp(partial(mixer_core, seg_ids=seg_ids, block_len=SPAN), proj_x[:, chan_cut], proj_bc, proj_dt[:, head_cut], conv_x[layer_index][:, chan_cut], bias_x[layer_index][chan_cut], conv_bc[layer_index], bias_bc[layer_index], dt_bias[layer_index][head_cut], a_log[layer_index][head_cut], d_skip[layer_index][head_cut])
            outputs_list.append(mixed_part)
            backs.append(back_part)
        mixed = jnp.concatenate(outputs_list, axis=1)
        gated = mixed * jax.nn.silu(gate_raw)
        scale_gate = lax.rsqrt(lax.optimization_barrier(jnp.mean(gated * gated, axis=1)) + epsilon)
        normed_out = (gated * scale_gate[:, None] * gate_gain[layer_index][None, :]).astype(jnp.bfloat16)
        branch = jnp.dot(normed_out, w_out[layer_index], preferred_element_type=jnp.float32) * live[:, None]
        stored.append((stream, scale_pre, normed, gate_raw, mixed, gated, scale_gate, normed_out, backs))
        stream = stream + branch
    result = stream.astype(jnp.bfloat16)
    grads = [[None] * LAYERS for name_index in range(14)]
    stream_grad = cotan.astype(jnp.float32)
    for layer_index in reversed(range(LAYERS)):
        stream_in, scale_pre, normed, gate_raw, mixed, gated, scale_gate, normed_out, backs = stored[layer_index]
        branch_grad = (stream_grad * live[:, None]).astype(jnp.bfloat16)
        grads[4][layer_index] = jnp.einsum('gi,gd->id', normed_out, branch_grad, preferred_element_type=jnp.float32)
        d_normed_out = jnp.einsum('gd,id->gi', branch_grad, w_out[layer_index], preferred_element_type=jnp.float32)
        gain_row = gate_gain[layer_index]
        grads[12][layer_index] = lax.optimization_barrier(jnp.sum(d_normed_out * gated * scale_gate[:, None], axis=0))
        inner_dot = lax.optimization_barrier(jnp.sum(d_normed_out * gain_row[None, :] * gated, axis=1))
        d_gated = scale_gate[:, None] * gain_row[None, :] * d_normed_out - gated * (scale_gate ** 3 * inner_dot / INNER)[:, None]
        sigmoid_gate = jax.nn.sigmoid(gate_raw)
        d_mixed = d_gated * gate_raw * sigmoid_gate
        d_gate_raw = d_gated * mixed * sigmoid_gate * (1.0 + gate_raw * (1.0 - sigmoid_gate))
        pieces = [backs[group_index](d_mixed[:, group_index * inner_part:(group_index + 1) * inner_part]) for group_index in range(N_TENSOR)]
        d_gate_b = d_gate_raw.astype(jnp.bfloat16)
        d_x_b = jnp.concatenate([piece[0] for piece in pieces], axis=1).astype(jnp.bfloat16)
        d_dt_b = jnp.concatenate([piece[2] for piece in pieces], axis=1).astype(jnp.bfloat16)
        d_bc_parts = [piece[1].astype(jnp.bfloat16) for piece in pieces]
        grads[0][layer_index] = jnp.einsum('gd,gk->dk', normed, d_gate_b, preferred_element_type=jnp.float32)
        grads[1][layer_index] = jnp.einsum('gd,gk->dk', normed, d_x_b, preferred_element_type=jnp.float32)
        grads[2][layer_index] = jnp.einsum('gd,gk->dk', normed, d_dt_b, preferred_element_type=jnp.float32)
        grad_bc = jnp.zeros((D, 2 * STATE), jnp.float32)
        d_normed = jnp.einsum('gk,dk->gd', d_gate_b, w_z[layer_index], preferred_element_type=jnp.float32)
        d_normed = d_normed + jnp.einsum('gk,dk->gd', d_x_b, w_x[layer_index], preferred_element_type=jnp.float32)
        d_normed = d_normed + jnp.einsum('gk,dk->gd', d_dt_b, w_dt[layer_index], preferred_element_type=jnp.float32)
        for part_bc in d_bc_parts:
            grad_bc = grad_bc + jnp.einsum('gd,gk->dk', normed, part_bc, preferred_element_type=jnp.float32)
            d_normed = d_normed + jnp.einsum('gk,dk->gd', part_bc, w_bc[layer_index], preferred_element_type=jnp.float32)
        grads[3][layer_index] = grad_bc
        grads[5][layer_index] = jnp.concatenate([piece[3] for piece in pieces], axis=1)
        grads[6][layer_index] = reduce_sum([piece[5] for piece in pieces])
        grads[7][layer_index] = jnp.concatenate([piece[4] for piece in pieces], axis=0)
        grads[8][layer_index] = reduce_sum([piece[6] for piece in pieces])
        grads[9][layer_index] = jnp.concatenate([piece[7] for piece in pieces], axis=0)
        grads[10][layer_index] = jnp.concatenate([piece[8] for piece in pieces], axis=0)
        grads[11][layer_index] = jnp.concatenate([piece[9] for piece in pieces], axis=0)
        pre_row = pre_gain[layer_index]
        grads[13][layer_index] = lax.optimization_barrier(jnp.sum(d_normed * stream_in * scale_pre[:, None], axis=0))
        pre_dot = lax.optimization_barrier(jnp.mean(d_normed * pre_row[None, :] * stream_in, axis=1))
        stream_grad = stream_grad + scale_pre[:, None] * pre_row[None, :] * d_normed - stream_in * (scale_pre ** 3 * pre_dot)[:, None]
    stacked = tuple((jnp.stack(entry, axis=0) for entry in grads))
    return (result, stream_grad, stacked)

def reduce_sum(arrays):
    total = arrays[0]
    for other in arrays[1:]:
        total = total + other
    return total

def reference(hidden_in, w_z, w_x, w_dt, w_bc, w_out, conv_x, conv_bc, bias_x, bias_bc, dt_bias, a_log, d_skip, gate_gain, pre_gain, seq_lengths, cotangent):
    params = (w_z, w_x, w_dt, w_bc, w_out, conv_x, conv_bc, bias_x, bias_bc, dt_bias, a_log, d_skip, gate_gain, pre_gain)

    def visit(totals, items):
        hidden, cotan, lengths = items
        result, stream_grad, grads = group_pass(hidden, cotan, lengths, params)
        return (tuple((left + right for left, right in zip(totals, grads))), (result, stream_grad))
    zeros = tuple((jnp.zeros(param.shape, jnp.float32) for param in params))
    totals, (results, stream_grads) = lax.scan(visit, zeros, (hidden_in.reshape(GROUPS, TOK_GRP, D), cotangent.reshape(GROUPS, TOK_GRP, D), seq_lengths))
    return (results.reshape(TOKENS, D), stream_grads.reshape(TOKENS, D), totals[0], totals[1], totals[2], totals[3], totals[4], totals[5], totals[6], totals[7], totals[8], totals[9], totals[10], totals[11], totals[12], totals[13])
```

```python
from functools import partial

import jax
import jax.numpy as jnp
from jax import lax
from jax.sharding import PartitionSpec as P

INNER = 2048
SPAN = 128
LAYERS = 2
SLOTS = 4


epsilon = 1e-05
highest = lax.Precision.HIGH


def segment_ids(lengths, count):
    ends = jnp.cumsum(lengths)
    places = jnp.arange(count, dtype=jnp.int32)
    return jnp.sum((places[:, None] >= ends[None, :]).astype(jnp.int32), axis=1)


def causal_conv(values, kernel, offset, seg_ids):
    total = offset[None, :] + kernel[-1][None, :] * values
    for back_step in range(1, kernel.shape[0]):
        moved = jnp.concatenate(
            [jnp.zeros((back_step, values.shape[1]), jnp.float32), values[:-back_step]], axis=0
        )
        moved_ids = jnp.concatenate([jnp.full((back_step,), -1, jnp.int32), seg_ids[:-back_step]])
        same_seq = (moved_ids == seg_ids).astype(jnp.float32)
        total = total + kernel[-1 - back_step][None, :] * moved * same_seq[:, None]
    return total


def state_scan(channels, step_sizes, decay_rate, b_mat, c_mat, seg_ids, block_len):
    count, nheads = step_sizes.shape
    head_width = channels.shape[1] // nheads
    nstate = b_mat.shape[1]
    nblocks = count // block_len
    xs = channels.reshape(nblocks, block_len, nheads, head_width)
    steps_h = jnp.transpose(step_sizes.reshape(nblocks, block_len, nheads), (0, 2, 1))
    bs = b_mat.reshape(nblocks, block_len, nstate)
    cs = c_mat.reshape(nblocks, block_len, nstate)
    ids = seg_ids.reshape(nblocks, block_len)
    cumul = jnp.cumsum(steps_h * decay_rate[None, :, None], axis=2)
    scores = jnp.einsum("cin,cjn->cij", cs, bs, precision=highest)
    places = jnp.arange(block_len)
    allowed = (ids[:, :, None] == ids[:, None, :]) & (places[:, None] >= places[None, :])[None]
    spread = cumul[:, :, :, None] - cumul[:, :, None, :]
    decay = jnp.exp(jnp.where(allowed[:, None, :, :], spread, -1e30))
    mixing = scores[:, None, :, :] * decay * steps_h[:, :, None, :]
    inside = jnp.einsum("chij,cjhp->cihp", mixing, xs, precision=highest)
    last_ids = ids[:, -1]
    tail = (
        jnp.exp(jnp.where((ids == last_ids[:, None])[:, None, :], cumul[:, :, -1:] - cumul, -1e30))
        * steps_h
    )
    fresh = jnp.einsum("chj,cjn,cjhp->chpn", tail, bs, xs, precision=highest)
    prev_ids = jnp.concatenate([jnp.full((1,), -1, jnp.int32), last_ids[:-1]])
    keep_flag = (last_ids == prev_ids).astype(jnp.float32)
    carry_decay = jnp.exp(cumul[:, :, -1]) * keep_flag[:, None]

    def advance(state, inputs):
        factor, newer = inputs
        return (factor[:, None, None] * state + newer, state)

    _, before = lax.scan(
        advance, jnp.zeros((nheads, head_width, nstate), jnp.float32), (carry_decay, fresh), unroll=True
    )
    reach = jnp.exp(cumul) * (ids == prev_ids[:, None]).astype(jnp.float32)[:, None, :]
    outside = (
        jnp.einsum("cin,chpn->cihp", cs, before, precision=highest)
        * jnp.transpose(reach, (0, 2, 1))[..., None]
    )
    return (inside + outside).reshape(count, nheads * head_width)


def mixer_core(
    proj_x,
    proj_bc,
    proj_dt,
    conv_x,
    bias_x,
    conv_bc,
    bias_bc,
    dt_bias,
    a_log,
    d_skip,
    seg_ids,
    block_len,
):
    x_conv = jax.nn.silu(causal_conv(proj_x, conv_x, bias_x, seg_ids))
    bc_conv = jax.nn.silu(causal_conv(proj_bc, conv_bc, bias_bc, seg_ids))
    nstate = bc_conv.shape[1] // 2
    step_sizes = jax.nn.softplus(proj_dt + dt_bias[None, :])
    head_width = x_conv.shape[1] // step_sizes.shape[1]
    scanned = state_scan(
        x_conv,
        step_sizes,
        -jnp.exp(a_log),
        bc_conv[:, :nstate],
        bc_conv[:, nstate:],
        seg_ids,
        block_len,
    )
    return scanned + jnp.repeat(d_skip, head_width)[None, :] * x_conv


def fetch_weights(w_z, w_x, w_dt, w_bc, w_out, layer_index):
    shared = lax.all_gather(w_bc[layer_index], "tensor", axis=0, tiled=True)
    packed = jnp.concatenate(
        [w_z[layer_index], w_x[layer_index], w_out[layer_index].T, shared, w_dt[layer_index]],
        axis=1,
    )
    return lax.all_gather(packed, "dp", axis=0, tiled=True)


def per_device(
    hidden_in,
    w_z,
    w_x,
    w_dt,
    w_bc,
    w_out,
    conv_x,
    conv_bc,
    bias_x,
    bias_bc,
    dt_bias,
    a_log,
    d_skip,
    gate_gain,
    pre_gain,
    seq_lengths,
    cotangent,
):
    tok_rows = hidden_in.shape[0]
    group_rows = tok_rows * lax.axis_size("tensor")
    seg_ids = segment_ids(seq_lengths[0], group_rows)
    live_all = (seg_ids < SLOTS).astype(jnp.float32)
    live_rows = lax.dynamic_slice_in_dim(live_all, lax.axis_index("tensor") * tok_rows, tok_rows, 0)
    inner_part = w_z.shape[2]
    head_part = w_dt.shape[2]
    stream = hidden_in.astype(jnp.float32)
    bc_part = w_bc.shape[2]
    out_stop = 3 * inner_part
    bc_stop = out_stop + bc_part
    stored = []
    for layer_index in range(LAYERS):
        weight_set = fetch_weights(w_z, w_x, w_dt, w_bc, w_out, layer_index)
        scale_pre = lax.rsqrt(jnp.mean(stream * stream, axis=1) + epsilon)
        normed = (stream * scale_pre[:, None] * pre_gain[layer_index][None, :]).astype(jnp.bfloat16)
        normed_all = lax.all_gather(normed, "tensor", axis=0, tiled=True)
        main_matrix = weight_set[:, : 2 * inner_part]
        side_matrix = weight_set[:, out_stop:]
        out_matrix = weight_set[:, 2 * inner_part : out_stop]
        projected = jnp.dot(normed_all, main_matrix, preferred_element_type=jnp.float32)
        side = jnp.dot(normed_all, side_matrix, preferred_element_type=jnp.float32)
        gate_raw = projected[:, :inner_part]
        proj_x = projected[:, inner_part:]
        proj_bc = side[:, :bc_part]
        proj_dt = side[:, bc_part:]
        mixed, back_fn = jax.vjp(
            partial(mixer_core, seg_ids=seg_ids, block_len=SPAN),
            proj_x,
            proj_bc,
            proj_dt,
            conv_x[layer_index],
            bias_x[layer_index],
            conv_bc[layer_index],
            bias_bc[layer_index],
            dt_bias[layer_index],
            a_log[layer_index],
            d_skip[layer_index],
        )
        gated = mixed * jax.nn.silu(gate_raw)
        square_sum = lax.psum(jnp.sum(gated * gated, axis=1), "tensor")
        scale_gate = lax.rsqrt(square_sum / INNER + epsilon)
        normed_out = (gated * scale_gate[:, None] * gate_gain[layer_index][None, :]).astype(
            jnp.bfloat16
        )
        branch = (
            lax.psum_scatter(
                jnp.einsum(
                    "gi,di->gd", normed_out, out_matrix, preferred_element_type=jnp.float32
                ).astype(jnp.bfloat16),
                "tensor",
                scatter_dimension=0,
                tiled=True,
            ).astype(jnp.float32)
            * live_rows[:, None]
        )
        stored.append(
            (
                stream,
                scale_pre,
                normed_all,
                gate_raw,
                mixed,
                gated,
                scale_gate,
                normed_out,
                back_fn,
                (main_matrix, side_matrix, out_matrix),
            )
        )
        stream = stream + branch
    hidden_out = stream.astype(jnp.bfloat16)
    grads = [[None] * LAYERS for name_index in range(14)]
    small = []
    stream_grad = cotangent.astype(jnp.float32)
    for layer_index in reversed(range(LAYERS)):
        (
            stream_in,
            scale_pre,
            normed_all,
            gate_raw,
            mixed,
            gated,
            scale_gate,
            normed_out,
            back_fn,
            weight_set,
        ) = stored[layer_index]
        main_matrix, side_matrix, out_matrix = weight_set
        branch_grad = (stream_grad * live_rows[:, None]).astype(jnp.bfloat16)
        grad_all = lax.all_gather(branch_grad, "tensor", axis=0, tiled=True)
        grad_out = jnp.einsum("gd,gi->di", grad_all, normed_out, preferred_element_type=jnp.float32)
        d_normed_out = jnp.einsum(
            "gd,di->gi", grad_all, out_matrix, preferred_element_type=jnp.float32
        )
        gain_row = gate_gain[layer_index]
        grad_gain = jnp.sum(d_normed_out * gated * scale_gate[:, None], axis=0)
        inner_dot = lax.psum(jnp.sum(d_normed_out * gain_row[None, :] * gated, axis=1), "tensor")
        d_gated = (
            scale_gate[:, None] * gain_row[None, :] * d_normed_out
            - gated * (scale_gate**3 * inner_dot / INNER)[:, None]
        )
        sigmoid_gate = jax.nn.sigmoid(gate_raw)
        d_mixed = d_gated * gate_raw * sigmoid_gate
        d_gate_raw = d_gated * mixed * sigmoid_gate * (1.0 + gate_raw * (1.0 - sigmoid_gate))
        pieces = back_fn(d_mixed)
        d_main = jnp.concatenate([d_gate_raw, pieces[0]], axis=1).astype(jnp.bfloat16)
        d_side = jnp.concatenate([pieces[1], pieces[2]], axis=1).astype(jnp.bfloat16)
        out_owned = lax.psum_scatter(
            grad_out.astype(jnp.bfloat16), "dp", scatter_dimension=0, tiled=True
        )
        grad_main = jnp.einsum("gd,gk->dk", normed_all, d_main, preferred_element_type=jnp.float32)
        grad_side = jnp.einsum("gd,gk->dk", normed_all, d_side, preferred_element_type=jnp.float32)
        owned = lax.psum_scatter(
            jnp.concatenate(
                [grad_main.astype(jnp.bfloat16), grad_side.astype(jnp.bfloat16)], axis=1
            ),
            "dp",
            scatter_dimension=0,
            tiled=True,
        ).astype(jnp.float32)
        grads[0][layer_index] = owned[:, :inner_part]
        grads[1][layer_index] = owned[:, inner_part : 2 * inner_part]
        grads[2][layer_index] = owned[:, 2 * inner_part + bc_part :]
        grads[3][layer_index] = lax.psum_scatter(
            owned[:, 2 * inner_part : 2 * inner_part + bc_part],
            "tensor",
            scatter_dimension=0,
            tiled=True,
        )
        grads[4][layer_index] = out_owned.T.astype(jnp.float32)
        d_normed = lax.psum_scatter(
            (
                jnp.einsum("gk,dk->gd", d_main, main_matrix, preferred_element_type=jnp.float32)
                + jnp.einsum("gk,dk->gd", d_side, side_matrix, preferred_element_type=jnp.float32)
            ).astype(jnp.bfloat16),
            "tensor",
            scatter_dimension=0,
            tiled=True,
        ).astype(jnp.float32)
        pre_row = pre_gain[layer_index]
        grad_pre = jnp.sum(d_normed * stream_in * scale_pre[:, None], axis=0)
        pre_dot = jnp.mean(d_normed * pre_row[None, :] * stream_in, axis=1)
        stream_grad = (
            stream_grad
            + scale_pre[:, None] * pre_row[None, :] * d_normed
            - stream_in * (scale_pre**3 * pre_dot)[:, None]
        )
        for place, value in (
            (6, pieces[5]),
            (8, pieces[6]),
            (13, grad_pre),
            (5, pieces[3]),
            (7, pieces[4]),
            (9, pieces[7]),
            (10, pieces[8]),
            (11, pieces[9]),
            (12, grad_gain),
        ):
            small.append((place, layer_index, value))
    small.sort(key=lambda entry: entry[0] not in (6, 8, 13))
    flat = lax.psum(jnp.concatenate([entry[2].reshape(-1) for entry in small]), "dp")
    shared_size = sum(entry[2].size for entry in small if entry[0] in (6, 8, 13))
    shared_flat = lax.psum(flat[:shared_size], "tensor")
    offset = 0
    for place, layer_index, value in small:
        source = shared_flat if place in (6, 8, 13) else flat
        grads[place][layer_index] = source[offset : offset + value.size].reshape(value.shape)
        offset += value.size
    stacked = [jnp.stack(entry, axis=0) for entry in grads]
    return (
        hidden_out,
        stream_grad,
        stacked[0],
        stacked[1],
        stacked[2],
        stacked[3],
        stacked[4],
        stacked[5],
        stacked[6],
        stacked[7],
        stacked[8],
        stacked[9],
        stacked[10],
        stacked[11],
        stacked[12],
        stacked[13],
    )


def solution(mesh):
    return jax.shard_map(
        per_device,
        mesh=mesh,
        in_specs=(
            P(("dp", "tensor"), None),
            P(None, "dp", "tensor"),
            P(None, "dp", "tensor"),
            P(None, "dp", "tensor"),
            P(None, ("dp", "tensor"), None),
            P(None, "tensor", "dp"),
            P(None, None, "tensor"),
            P(),
            P(None, "tensor"),
            P(),
            P(None, "tensor"),
            P(None, "tensor"),
            P(None, "tensor"),
            P(None, "tensor"),
            P(),
            P("dp", None),
            P(("dp", "tensor"), None),
        ),
        out_specs=(
            P(("dp", "tensor"), None),
            P(("dp", "tensor"), None),
            P(None, "dp", "tensor"),
            P(None, "dp", "tensor"),
            P(None, "dp", "tensor"),
            P(None, ("dp", "tensor"), None),
            P(None, "tensor", "dp"),
            P(None, None, "tensor"),
            P(),
            P(None, "tensor"),
            P(),
            P(None, "tensor"),
            P(None, "tensor"),
            P(None, "tensor"),
            P(None, "tensor"),
            P(),
        ),
        check_vma=False,
    )
```
